256 devices in a mesh: leaf: 256 (over y, z, x, core).
Axes of the slice: x: 4, y: 4, z: 8, core: 2. Of those that a mesh axis runs over, the one named last changes fastest.
Arguments:
- points: bfloat16 [64, 1048576], P(None, 'leaf'), may hold values from -0.8 to 0.8
- leaf_order: int32 [1048576], P('leaf'), may hold values from 0 to 4095, as said below
- near_pairs: int32 [2048, 4], P('leaf'), may hold values from -1 to 2047, as said below
- solution: float32 [64, 1048576], P(None, 'leaf'), may hold values from -6 to 6
- residual: float32 [64, 1048576], P(None, 'leaf'), may hold values from -44 to 44
- direction: float32 [64, 1048576], P(None, 'leaf'), may hold values from -44 to 44
- skeleton_basis: bfloat16 [256, 1048576], P(None, 'leaf'), may hold values from -0.1875 to 0.1875
- transfers: float32 [1280, 256, 256], P('leaf'), may hold values from -0.375 to 0.375
- couplings: float32 [6, 256, 256], replicated, may hold values from -0.375 to 0.375
Outputs:
- new_solution: float32 [64, 1048576], P(None, 'leaf')
- new_residual: float32 [64, 1048576], P(None, 'leaf')
- new_direction: float32 [64, 1048576], P(None, 'leaf')
The draws below stay inside these ranges and needn't reach their ends.
Inputs may be any that keep to these rules, and one draw needn't show every extreme that they name: `leaf_order`: the entries of each slab's 4096 positions are a permutation of 0 to 4095. `near_pairs`: row a lists 4 different later leaves: the first is always a + 1, the others lie among a + 2 to a + 8; -1 stands where that leaf would lie past the last leaf.
All inputs are finite; a program needn't handle non-finite values.
Results may differ from the reference program's by a relative error of at most 0.0034.
The reference program's roundings to bfloat16 on the way count: a program that leaves them out, or rounds other values in their place, can miss the bound.
Values may be sent and summed in bfloat16 or wider, within the bound.
No kernel may reach another device: no remote copies, remote signals or barrier semaphores. Data moves between devices by JAX's collectives and lax.ppermute only.
A program may use at most 128 MiB of HBM per device.

```python
import jax
import jax.numpy as jnp
from jax import lax

DIM = 64
LEAF = 512
RANK = 256
NRHS = 64
LEAF_DEV = 8
NPAIR = 4
LEVELS = 5
PTS_DEV = 4096
LEAVES = 2048
NPTS = 1048576
STACK = 1280
N_LEAF = 256


def order_helper(key):
    keys = jax.random.split(jax.random.fold_in(key, 7), NPTS // PTS_DEV)
    perms = jax.vmap(lambda one_key: jax.random.permutation(one_key, PTS_DEV))(keys)
    return perms.astype(jnp.int32)


def draw_leaf_order(key, part):
    return order_helper(key).reshape(-1)


def draw_points(key, part):
    perms = order_helper(key)
    inverse = jnp.argsort(perms, axis=1).astype(jnp.int32)
    blocks = jnp.arange(NPTS // PTS_DEV, dtype=jnp.int32)[:, None] * PTS_DEV
    leaf_ids = ((blocks + inverse) // LEAF).reshape(-1)
    salted = jax.random.fold_in(key, 9)
    center_key, noise_key = jax.random.split(salted, 2)
    centers = jnp.clip(jax.random.normal(center_key, (DIM, LEAVES), jnp.float32), -5.0, 5.0) / 32.0
    noise = jnp.clip(jax.random.normal(noise_key, (DIM, NPTS), jnp.float32), -5.0, 5.0) / 8.0
    coords = jnp.take(centers, leaf_ids, axis=1) + noise
    return coords.astype(jnp.bfloat16)


def draw_near_pairs(key, part):
    keys = jax.random.split(jax.random.fold_in(key, 3), LEAVES)
    perms = jax.vmap(lambda one_key: jax.random.permutation(one_key, LEAF_DEV - 1))(keys).astype(jnp.int32)
    offsets = jnp.concatenate([jnp.ones((LEAVES, 1), jnp.int32), perms[:, :NPAIR - 1] + 2], axis=1)
    partner = jnp.arange(LEAVES, dtype=jnp.int32)[:, None] + offsets
    return jnp.where(partner < LEAVES, partner, -1).astype(jnp.int32)


def state_draw(key, salt):
    salted = jax.random.fold_in(key, salt)
    value_key, spread_key, column_key = jax.random.split(salted, 3)
    where_at = jnp.arange(NPTS, dtype=jnp.float32) / NPTS
    ramp = jnp.sqrt(1.0 + 2.0 * where_at)
    spread = jnp.exp(jax.random.uniform(spread_key, (NPTS,), jnp.float32, -1.15, 1.15))
    columns = jnp.exp(jax.random.uniform(column_key, (NRHS, 1), jnp.float32, -0.55, 0.55))
    values = jnp.clip(jax.random.normal(value_key, (NRHS, NPTS), jnp.float32), -4.5, 4.5)
    return (values * columns * (ramp * spread)[None, :]).astype(jnp.float32)


def coherent_draw(key, salt):
    salted = jax.random.fold_in(key, salt)
    value_key, spread_key, column_key, level_key, sign_key = jax.random.split(salted, 5)
    where_at = jnp.arange(NPTS, dtype=jnp.float32) / NPTS
    ramp = jnp.sqrt(1.0 + 2.0 * where_at)
    spread = jnp.exp(jax.random.uniform(spread_key, (NPTS,), jnp.float32, -1.15, 1.15))
    columns = jnp.exp(jax.random.uniform(column_key, (NRHS, 1), jnp.float32, -0.55, 0.55))
    levels_per_leaf = jax.random.uniform(level_key, (NRHS, LEAVES), jnp.float32, 0.5, 1.5)
    signs = (jax.random.randint(sign_key, (NRHS, 1), 0, 2) * 2 - 1).astype(jnp.float32)
    leaf_part = jnp.repeat(levels_per_leaf, LEAF, axis=1) * signs
    own_part = jnp.clip(jax.random.normal(value_key, (NRHS, NPTS), jnp.float32), -4.5, 4.5)
    values = 0.8 * own_part + 0.6 * leaf_part
    return (values * columns * (ramp * spread)[None, :]).astype(jnp.float32)


def draw_residual(key, part):
    return state_draw(key, 21)


def draw_direction(key, part):
    mixed = 0.8 * state_draw(key, 21) + 0.6 * coherent_draw(key, 22)
    return jnp.clip(mixed, -44.0, 44.0).astype(jnp.float32)


def levels(stream_key, extent, pieces, smallest, largest):
    def one(position, blocks):
        heights = jax.random.uniform(jax.random.fold_in(jax.random.fold_in(stream_key, 6), position), (blocks,), jnp.float32, smallest / len(pieces), largest / len(pieces))
        return jnp.repeat(jnp.exp(heights), extent[position] // blocks).reshape((-1,) + (1,) * (len(extent) - position - 1))

    level = one(*pieces[0])
    for cut in pieces[1:]:
        level = level * one(*cut)
    return level


def bell_draw(own_key, dims, width, bound, shards=(), held_as=jnp.bfloat16):
    result = jax.random.normal(own_key, dims, jnp.float32) * width
    if len(shards) > 0:
        result = levels(own_key, dims, shards, -0.22, 0.18) * result
    return jnp.clip(result, min=-bound, max=bound).astype(held_as)


def setup_inputs(seed: int = 0) -> dict:
    key_list = jax.random.split(jax.random.key(seed), 10)
    points = draw_points(jax.random.fold_in(key_list[9], 71), 0)
    leaf_order = draw_leaf_order(jax.random.fold_in(key_list[9], 71), 0)
    near_pairs = draw_near_pairs(jax.random.fold_in(key_list[9], 71), 0)
    solution = bell_draw(key_list[3], (NRHS, NPTS), 1.0, 6.0, ((1, 256),), jnp.float32)
    residual = draw_residual(jax.random.fold_in(key_list[9], 71), 0)
    direction = draw_direction(jax.random.fold_in(key_list[9], 71), 0)
    skeleton_basis = bell_draw(key_list[6], (RANK, NPTS), (PTS_DEV // 4) ** -0.5, 0.1875, ((1, 256),))
    transfers = bell_draw(key_list[7], (STACK, RANK, RANK), RANK ** -0.5, 0.375, ((0, 256),), jnp.float32)
    couplings = bell_draw(key_list[8], (LEVELS + 1, RANK, RANK), RANK ** -0.5, 0.375, (), jnp.float32)
    return {"points": points, "leaf_order": leaf_order, "near_pairs": near_pairs, "solution": solution, "residual": residual, "direction": direction, "skeleton_basis": skeleton_basis, "transfers": transfers, "couplings": couplings}


SHARPNESS = 2.0
EPSILON = 1e-6
HIGHEST = lax.Precision.HIGHEST


def couple(level_total, weights):
    halfway = jnp.matmul(level_total, weights, precision=HIGHEST)
    return jnp.matmul(halfway, jnp.swapaxes(weights, -1, -2), precision=HIGHEST)


def near_field(tree_points, p_half, near_pairs):
    leaf_points = tree_points.reshape(DIM, LEAVES, LEAF).astype(jnp.float32)
    leaf_values = p_half.reshape(NRHS, LEAVES, LEAF).astype(jnp.float32)
    squares = jnp.sum(leaf_points * leaf_points, axis=0)
    is_valid = near_pairs >= 0
    partner_ids = jnp.where(is_valid, near_pairs, 0).astype(jnp.int32)
    valid_int = is_valid.astype(jnp.int32)
    pair_totals = jnp.sum(valid_int, axis=1) + jnp.zeros((LEAVES,), jnp.int32).at[partner_ids.reshape(-1)].add(valid_int.reshape(-1))
    valid_float = is_valid.astype(jnp.float32)

    def visit_leaf(accum, leaf_index):
        row_ids = lax.dynamic_index_in_dim(partner_ids, leaf_index, 0, keepdims=False)
        row_weights = lax.dynamic_index_in_dim(valid_float, leaf_index, 0, keepdims=False)
        own_total = lax.dynamic_index_in_dim(pair_totals, leaf_index, 0, keepdims=False)
        others = jnp.concatenate([leaf_index[None].astype(jnp.int32), row_ids])
        source_weight = jnp.concatenate([(1 + own_total).astype(jnp.float32)[None], row_weights])
        other_weight = jnp.concatenate([jnp.zeros((1,), jnp.float32), row_weights])
        source_pts = lax.dynamic_index_in_dim(leaf_points, leaf_index, 1, keepdims=False)
        source_sq = lax.dynamic_index_in_dim(squares, leaf_index, 0, keepdims=False)
        source_val = lax.dynamic_index_in_dim(leaf_values, leaf_index, 1, keepdims=False)
        other_pts = jnp.take(leaf_points, others, axis=1)
        other_sq = jnp.take(squares, others, axis=0)
        other_val = jnp.take(leaf_values, others, axis=1)
        cross_dot = jnp.einsum("dk,dnj->nkj", source_pts, other_pts)
        distance = source_sq[None, :, None] + other_sq[:, None, :] - 2.0 * cross_dot
        kernel_tile = lax.optimization_barrier(jnp.exp(-SHARPNESS * distance).astype(jnp.bfloat16)).astype(jnp.float32)
        to_source = jnp.einsum("nkj,rnj->nrk", kernel_tile, other_val)
        to_source = jnp.sum(to_source * source_weight[:, None, None], axis=0)
        to_other = jnp.einsum("nkj,rk->rnj", kernel_tile, source_val) * other_weight[None, :, None]
        accum = accum.at[:, leaf_index, :].add(to_source)
        accum = accum.at[:, others, :].add(to_other)
        return accum, None

    start = jnp.zeros((NRHS, LEAVES, LEAF), jnp.float32)
    accum = lax.scan(visit_leaf, start, jnp.arange(LEAVES, dtype=jnp.int32))[0]
    return accum.reshape(NRHS, NPTS)


def far_field(p_half, skeleton_basis, transfers, couplings):
    slab_values = p_half.reshape(NRHS, N_LEAF, PTS_DEV).astype(jnp.float32)
    slab_basis = skeleton_basis.reshape(RANK, N_LEAF, PTS_DEV).astype(jnp.float32)
    slab_transfers = transfers.reshape(N_LEAF, LEVELS, RANK, RANK)
    level_skel = jnp.einsum("rsi,csi->src", slab_values, slab_basis)
    skeletons = [level_skel]
    for level_idx in range(LEVELS):
        level_skel = jnp.einsum("src,scd->srd", level_skel, slab_transfers[:, level_idx], precision=HIGHEST)
        skeletons.append(level_skel)
    top_total = jnp.sum(skeletons[LEVELS], axis=0)
    descent = jnp.broadcast_to(couple(top_total, couplings[LEVELS]), (N_LEAF, NRHS, RANK))
    for level_idx in reversed(range(LEVELS)):
        group = 2 ** (level_idx + 1)
        grouped = jnp.sum(skeletons[level_idx].reshape(N_LEAF // group, group, NRHS, RANK), axis=1)
        level_total = jnp.repeat(grouped, group, axis=0)
        descent = jnp.einsum("src,sdc->srd", descent, slab_transfers[:, level_idx], precision=HIGHEST) + couple(level_total, couplings[level_idx])
    descent_half = lax.optimization_barrier(descent.astype(jnp.bfloat16)).astype(jnp.float32)
    far = jnp.einsum("src,csi->rsi", descent_half, slab_basis)
    return far.reshape(NRHS, NPTS)


def reference(points, leaf_order, near_pairs, solution, residual, direction, skeleton_basis, transfers, couplings):
    positions = jnp.arange(NPTS, dtype=jnp.int32)
    source_cols = ((positions // PTS_DEV) * PTS_DEV + leaf_order).astype(jnp.int32)
    tree_points = jnp.take(points, source_cols, axis=1)
    p_half = lax.optimization_barrier(direction.astype(jnp.bfloat16))
    near = near_field(tree_points, p_half, near_pairs)
    far = far_field(p_half, skeleton_basis, transfers, couplings)
    image = direction + near + far
    old_norm = jnp.sum(residual * residual, axis=1)
    curve_sum = jnp.sum(direction * image, axis=1)
    step_size = old_norm / (curve_sum + EPSILON)
    new_solution = solution + step_size[:, None] * direction
    new_residual = residual - step_size[:, None] * image
    new_norm = jnp.sum(new_residual * new_residual, axis=1)
    ratio = new_norm / (old_norm + EPSILON)
    new_direction = new_residual + ratio[:, None] * direction
    return new_solution, new_residual, new_direction
```

```python
import functools

import jax
import jax.numpy as jnp
from jax import lax
from jax.experimental import pallas as pl
from jax.experimental.pallas import tpu as pltpu
from jax.sharding import PartitionSpec as P

EPSILON = 1e-06
LOG2E = 1.4426950408889634
HIGHEST = lax.Precision.HIGHEST
LEAF = 512
DIM = 64
ROWS = 64
LANES = 128
NT = (((1,), (1,)), ((), ()))
VMEM = pl.BlockSpec(memory_space=pltpu.VMEM)
SMEM = pl.BlockSpec(memory_space=pltpu.SMEM)


def call(body, name, out_shape, in_specs, out_specs, scratch, limit, flops, args, aliases=None):
    return pl.pallas_call(
        body,
        name=name,
        out_shape=out_shape,
        in_specs=in_specs,
        out_specs=out_specs,
        scratch_shapes=scratch,
        input_output_aliases=aliases or {},
        compiler_params=pltpu.CompilerParams(vmem_limit_bytes=limit << 20),
        cost_estimate=pl.CostEstimate(flops=flops, bytes_accessed=1 << 20, transcendentals=0),
    )(*args)


def shape(dims, dtype=jnp.float32):
    return jax.ShapeDtypeStruct(dims, dtype)


def split_squares(x):
    total = -2.0 * jnp.sum(x * x, axis=0, keepdims=True)
    high = total.astype(jnp.bfloat16).astype(jnp.float32)
    rest = total - high
    middle = rest.astype(jnp.bfloat16).astype(jnp.float32)
    return high, middle, rest - middle


def side_rows(parts, first, width):
    row = lax.broadcasted_iota(jnp.int32, (8, width), 0)
    out = jnp.where(row < 6, 1.0, 0.0)
    for i, part in enumerate(parts):
        out = jnp.where(row == first + i, part, out)
    return out


def right_form(x, parts):
    width = x.shape[1]
    filler = jnp.zeros((LANES - DIM - 8, width), jnp.float32)
    rows = jnp.concatenate([4.0 * x, side_rows(parts, 3, width), filler], axis=0)
    return rows.astype(jnp.bfloat16)


def gather_body(order, points, direction, left, right, stack, rows, picked):
    count = points.shape[1]
    for c in range(0, count, LANES):
        block = points[:, c : c + LANES].astype(jnp.float32)
        rows[c : c + LANES, :DIM] = block.T
    stack[DIM:, :] = direction[...].astype(jnp.bfloat16)

    def pick(i, carry):
        for u in range(16):
            j = i * 16 + u
            picked[pl.ds(j, 1), :] = rows[pl.ds(order[j], 1), :]
        return carry

    lax.fori_loop(0, count // 16, pick, 0)
    for c in range(0, count, LANES):
        span = slice(c, c + LANES)
        x = picked[span, :DIM].T
        stack[:DIM, span] = x.astype(jnp.bfloat16)
        parts = split_squares(x)
        right[:, span] = right_form(x, parts)
        filler = jnp.zeros((LANES - DIM - 8, LANES), jnp.float32)
        rows_left = jnp.concatenate([x, side_rows(parts, 0, LANES), filler], axis=0)
        left[span, :] = rows_left.T.astype(jnp.bfloat16)


def gather(order, points, direction):
    count = points.shape[1]
    return call(
        gather_body,
        "gather",
        (
            shape((count, LANES), jnp.bfloat16),
            shape((LANES, count), jnp.bfloat16),
            shape((DIM + ROWS, count), jnp.bfloat16),
        ),
        [SMEM, VMEM, VMEM],
        (VMEM, VMEM, VMEM),
        [pltpu.VMEM((count, LANES), jnp.float32)] * 2,
        16,
        4 << 30,
        (order, points, direction),
    )


def prepare_body(stack, right):
    for c in range(0, stack.shape[1], LANES):
        span = slice(c, c + LANES)
        x = stack[:DIM, span].astype(jnp.float32)
        right[:, span] = right_form(x, split_squares(x))


def prepare(stack):
    return call(
        prepare_body,
        "prepare",
        shape((LANES, stack.shape[1]), jnp.bfloat16),
        [VMEM],
        VMEM,
        [],
        8,
        1 << 29,
        (stack,),
    )


def up_body(direction, basis, transfers, out):
    level = lax.dot_general(
        direction[...].astype(jnp.bfloat16), basis[...], NT, preferred_element_type=jnp.float32
    )
    out[0] = level
    for k in range(transfers.shape[0]):
        level = jnp.dot(level, transfers[k], precision=HIGHEST)
        out[k + 1] = level


def up(direction, basis, transfers):
    rank = basis.shape[0]
    depth = transfers.shape[0]
    return call(
        up_body,
        "up",
        shape((depth + 1, ROWS, rank)),
        [VMEM] * 3,
        VMEM,
        [],
        16,
        2 << 30,
        (direction, basis, transfers),
    )


def down_body(totals, top, transfers, couplings, out):
    depth = transfers.shape[0]

    def couple(total, weights):
        halfway = jnp.dot(total, weights, precision=HIGHEST)
        return lax.dot_general(halfway, weights, NT, precision=HIGHEST)

    descent = couple(top[...], couplings[depth])
    for k in reversed(range(depth)):
        descent = lax.dot_general(descent, transfers[k], NT, precision=HIGHEST) + couple(
            totals[k], couplings[k]
        )
    out[...] = descent.astype(jnp.bfloat16)


def down(totals, top, transfers, couplings):
    return call(
        down_body,
        "down",
        shape(top.shape, jnp.bfloat16),
        [VMEM] * 4,
        VMEM,
        [],
        16,
        2 << 30,
        (totals, top, transfers, couplings),
    )


def leaf_span(i):
    return pl.ds(pl.multiple_of(i * LEAF, LEAF), LEAF)


def tile(left, right, source, partner, out, slot):
    exponent = jnp.dot(
        left[leaf_span(source), :],
        right[:, leaf_span(partner)],
        preferred_element_type=jnp.float32,
    )
    out[slot] = jnp.exp2(exponent * LOG2E).astype(jnp.bfloat16)


def values(stack, i):
    return stack[DIM:, leaf_span(i)]


def self_body(pairs, prior, left, right, stack, acc, tiles, weight):
    leaves = pairs.shape[0]
    first = pairs[0, 0] - 1
    has_prior = first > 0
    for a in range(leaves):
        weight[a] = 1
    for a in range(leaves):
        for m in range(pairs.shape[1]):
            partner = pairs[a, m]
            slot = partner - first

            @pl.when(partner >= 0)
            def _(a=a):
                weight[a] += 1

            @pl.when((partner >= 0) & (slot < leaves))
            def _(slot=slot):
                weight[slot] += 1

            back = prior[a, m]

            @pl.when(has_prior & (back >= first))
            def _(back=back):
                weight[back - first] += 1

    half = acc.shape[0] // 2
    acc[half:] = jnp.zeros((half,) + acc.shape[1:], jnp.float32)

    def use(a, slot):
        product = jnp.dot(values(stack, a), tiles[slot], preferred_element_type=jnp.float32)
        acc[a] = product * weight[a].astype(jnp.float32)

    tile(left, right, 0, 0, tiles, 0)

    def step(t, carry):
        tile(left, right, t, t, tiles, lax.rem(t, 2))
        use(t - 1, lax.rem(t - 1, 2))
        return carry

    lax.fori_loop(1, leaves, step, 0)
    use(leaves - 1, (leaves - 1) % 2)


def self_terms(pairs, prior, left, right, stack):
    leaves = pairs.shape[0]
    return call(
        self_body,
        "self_terms",
        shape((2 * leaves, ROWS, LEAF)),
        [SMEM, SMEM, VMEM, VMEM, VMEM],
        VMEM,
        [pltpu.VMEM((2, LEAF, LEAF), jnp.bfloat16), pltpu.SMEM((leaves,), jnp.int32)],
        20,
        4 << 30,
        (pairs, prior, left, right, stack),
    )


def pair_body(crossing, piece, pieces, pairs, left, right, stack, other, given, *rest):
    if len(rest) == 4:
        acc, outgoing, tiles, listed = rest
    else:
        (acc, tiles, listed), outgoing = rest, None
    leaves, width = pairs.shape
    first = pairs[0, 0] - 1
    shift = leaves if crossing else 0

    def build(t, found):
        a = t // width
        slot = pairs[a, lax.rem(t, width)] - first
        wanted = (slot >= leaves) if crossing else ((slot >= 0) & (slot < leaves))

        @pl.when(wanted)
        def _():
            listed[0, found] = a
            listed[1, found] = slot - shift

        return found + jnp.where(wanted, 1, 0)

    found = lax.fori_loop(0, leaves * width, build, 0)
    low = found * piece // pieces
    high = found * (piece + 1) // pieces

    def use(t):
        a, b = listed[0, t], listed[1, t]
        block = tiles[lax.rem(t, 2)]
        acc[b + shift] += jnp.dot(values(stack, a), block, preferred_element_type=jnp.float32)
        acc[a] += lax.dot_general(
            values(other, b), block, NT, preferred_element_type=jnp.float32
        )

    def make(t):
        tile(left, right, listed[0, t], listed[1, t], tiles, lax.rem(t, 2))

    @pl.when(high > low)
    def _():
        make(low)

        def step(t, carry):
            make(t)
            use(t - 1)
            return carry

        lax.fori_loop(low + 1, high, step, 0)
        use(high - 1)

    if outgoing is not None:
        outgoing[...] = acc[leaves:].astype(jnp.bfloat16)


def pair_terms(crossing, piece, pieces, pairs, left, right, stack, other, acc):
    leaves, width = pairs.shape
    last = crossing and piece == pieces - 1
    outs = [shape(acc.shape)]
    if last:
        outs.append(shape((leaves, ROWS, LEAF), jnp.bfloat16))
    return call(
        functools.partial(pair_body, crossing, piece, pieces),
        "pairs_%d_%d" % (crossing, piece),
        tuple(outs),
        [SMEM] + [VMEM] * 5,
        (VMEM,) * len(outs),
        [
            pltpu.VMEM((2, LEAF, LEAF), jnp.bfloat16),
            pltpu.SMEM((2, leaves * width), jnp.int32),
        ],
        20,
        4 << 30,
        (pairs, left, right, stack, other, acc),
        {5: 0},
    )


def image_body(direction, residual, acc, arrived, half, basis, image, sums):
    leaves = arrived.shape[0]
    zero = jnp.zeros((ROWS, LANES), jnp.float32)
    curve = cross = energy = norm = zero
    for a in range(leaves):
        span = slice(a * LEAF, (a + 1) * LEAF)
        far = jnp.dot(half[...], basis[:, span], preferred_element_type=jnp.float32)
        d = direction[:, span]
        r = residual[:, span]
        value = d + (acc[a] + arrived[a].astype(jnp.float32)) + far
        image[:, span] = value
        for c in range(0, LEAF, LANES):
            part = slice(c, c + LANES)
            v, e, s = value[:, part], d[:, part], r[:, part]
            curve += e * v
            cross += s * v
            energy += v * v
            norm += s * s
    lane = lax.broadcasted_iota(jnp.int32, (ROWS, LANES), 1)
    packed = zero
    for i, total in enumerate((curve, cross, energy, norm)):
        packed = jnp.where(lane == i, jnp.sum(total, axis=1, keepdims=True), packed)
    rows = packed.T
    peers = sums.shape[0]
    upper = jnp.concatenate([rows[0:1], rows[1:2]], axis=1)
    lower = jnp.concatenate([rows[2:3], rows[3:4]], axis=1)
    sums[...] = jnp.broadcast_to(
        jnp.concatenate([upper, lower], axis=0)[None], (peers, 2, LANES)
    )


def image_terms(peers, direction, residual, acc, arrived, half, basis):
    return call(
        image_body,
        "image",
        (shape(direction.shape), shape((peers, 2, LANES))),
        [VMEM] * 6,
        (VMEM, VMEM),
        [],
        24,
        2 << 30,
        (direction, residual, acc, arrived, half, basis),
    )


def final_body(sums, solution, residual, direction, image, out_x, out_r, out_d):
    total = jnp.sum(sums[...], axis=0)
    columns = jnp.broadcast_to(total[:, None, :], (2, LANES, LANES))
    upper, lower = columns[0].T, columns[1].T
    curve, cross = upper[:ROWS], upper[ROWS:]
    energy, old = lower[:ROWS], lower[ROWS:]
    step = old / (curve + EPSILON)
    new = jnp.maximum(old - step * (2.0 * cross - step * energy), 0.0)
    ratio = new / (old + EPSILON)
    for c in range(0, solution.shape[1], LANES):
        span = slice(c, c + LANES)
        d = direction[:, span]
        out_x[:, span] = solution[:, span] + step * d
        left = residual[:, span] - step * image[:, span]
        out_r[:, span] = left
        out_d[:, span] = left + ratio * d


def final(sums, solution, residual, direction, image):
    peers = sums.shape[0]
    count = solution.shape[1]
    width = 1024
    block = pl.BlockSpec((ROWS, width), lambda i: (0, i))
    return pl.pallas_call(
        final_body,
        name="final",
        grid=(count // width,),
        out_shape=(shape(solution.shape),) * 3,
        in_specs=[pl.BlockSpec((peers, 2, LANES), lambda i: (0, 0, 0))] + [block] * 4,
        out_specs=(block,) * 3,
        compiler_params=pltpu.CompilerParams(vmem_limit_bytes=16 << 20),
        cost_estimate=pl.CostEstimate(flops=1 << 26, bytes_accessed=7 << 20, transcendentals=0),
    )(sums, solution, residual, direction, image)


def swapped(block, axis, apart):
    count = lax.axis_size(axis)
    return lax.ppermute(block, axis, [(i, i ^ (1 << apart)) for i in range(count)])


def passed_along(x, axis, by):
    peers = lax.axis_size(axis)
    pairs = [(i, i + by) for i in range(peers) if 0 <= i + by < peers]
    return lax.ppermute(x, axis, pairs)


def local(
    points,
    leaf_order,
    near_pairs,
    solution,
    residual,
    direction,
    skeleton_basis,
    transfers,
    couplings,
):
    peers = lax.axis_size("leaf")
    depth = transfers.shape[0]
    bits = peers.bit_length() - 1
    prior = passed_along(near_pairs, "leaf", 1)
    running = up(direction, skeleton_basis, transfers)
    left, right, stack = gather(leaf_order, points, direction)
    ahead = passed_along(stack, "leaf", -1)

    state = {}

    def near_piece(i):
        if i == 0:
            state["acc"] = self_terms(near_pairs, prior, left, right, stack)
        elif i <= 3:
            (state["acc"],) = pair_terms(
                0, i - 1, 3, near_pairs, left, right, stack, stack, state["acc"]
            )
        else:
            if i == 4:
                state["next"] = prepare(ahead)
            out = pair_terms(
                1, i - 4, 3, near_pairs, left, state["next"], stack, ahead, state["acc"]
            )
            state["acc"] = out[0]
            if len(out) > 1:
                state["outgoing"] = out[1]

    totals = []
    for bit in range(bits):
        running = running + swapped(running, "leaf", bit)
        if bit < depth:
            totals.append(running[0])
            running = running[1:]
        if bit < 7:
            near_piece(bit)
    top = running[0]
    arrived = passed_along(state["outgoing"], "leaf", 1)
    half = down(jnp.stack(totals), top, transfers, couplings)
    image, sums = image_terms(
        peers, direction, residual, state["acc"], arrived, half, skeleton_basis
    )
    gathered = lax.all_to_all(sums, "leaf", 0, 0, tiled=True)
    return final(gathered, solution, residual, direction, image)


def solution(mesh):
    in_specs = (
        P(None, "leaf"),
        P("leaf"),
        P("leaf", None),
        P(None, "leaf"),
        P(None, "leaf"),
        P(None, "leaf"),
        P(None, "leaf"),
        P("leaf", None, None),
        P(),
    )
    out_specs = (P(None, "leaf"), P(None, "leaf"), P(None, "leaf"))
    return jax.shard_map(local, mesh=mesh, in_specs=in_specs, out_specs=out_specs, check_vma=False)
```
